32 devices in a mesh: dom: 2 (over y), feat: 4 (over z), dp: 4 (over x, core).
Axes of the slice: x: 2, y: 2, z: 4, core: 2. Of those that a mesh axis runs over, the one named last changes fastest.
Arguments:
- layer_in: bfloat16 [32768, 2048], P(('dom', 'dp', 'feat')), parts along dimension 0, may hold values from -6 to 6
- grad_out: bfloat16 [32768, 2048], P(('dom', 'dp', 'feat')), parts along dimension 0, may hold values from -6 to 6
- in_proj: bfloat16 [2048, 256], replicated, may hold values from -0.125 to 0.125
- out_proj: bfloat16 [2048, 256], replicated, may hold values from -0.125 to 0.125
- queries: bfloat16 [2048, 65536], P(('dom', 'dp'), 'feat'), parts along dimension 0, may hold values from -0.00390625 to 0.00390625
- seq_ids: int32 [32, 1024], P(('dom', 'dp', 'feat')), parts along dimension 0, may hold values from 0 to 15, never falling along the last dimension, each value on 1 to 128 neighbouring positions
- valid_counts: int32 [512], P(('dom', 'dp', 'feat')), parts along dimension 0, may hold values from 16 to 128
- owner_order: int32 [2048], P(('dom', 'dp')), parts along dimension 0, may hold values from 0 to 1023, as said below
Outputs:
- scores: float32 [2048, 256], P(('dom', 'dp', 'feat')), parts along dimension 0
The draws below stay inside these ranges and needn't reach their ends.
There are 2 independent parts, one for each index of `dom`. The reference program is written for one: setup_inputs(seed, part) draws one part's arguments, and reference() takes and returns one part's arrays. A program takes and returns all parts, laid end to end along the dimension named above; an argument that names none is the same for every part. Nothing has to cross between parts.
Inputs may be any that keep to these rules, and one draw needn't show every extreme that they name: `seq_ids`: each row numbers the 16 sequences of one block in order, never falling; every number appears. `owner_order`: within each aligned block of 256 rows, a permutation of that block's row numbers.
All inputs are finite; a program needn't handle non-finite values.
Results may differ from the reference program's by a relative error of at most 0.005.
Values may be sent and summed in bfloat16 or wider, within the bound.
A program may use at most 64 MiB of HBM per device.

```python
import math
import jax
import jax.numpy as jnp
import numpy as np
from jax import lax

D = 2048
R = 256
FEATS = 65536
SEQ_DEV = 16
SEQ_LEN = 64
WIN = 128
TOK_DEV = 1024
GROUPS = 16
TOKENS = 16384
SEQUENCES = 256
Q_DP = 256
QUERIES = 1024


def draw_owner_order(key, part):
    blocks = QUERIES // Q_DP
    subkeys = jax.random.split(jax.random.fold_in(key, 17), blocks)

    def one_order(subkey):
        return jax.random.permutation(subkey, Q_DP).astype(jnp.int32)
    orders = jax.vmap(one_order)(subkeys)
    offsets = (jnp.arange(blocks, dtype=jnp.int32) * Q_DP)[:, None]
    return (orders + offsets).reshape(QUERIES).astype(jnp.int32)


def plant(drawn, rng, least, top_value):
    place = [jax.random.randint(jax.random.fold_in(rng, axis), (), 0, length) for axis, length in enumerate(drawn.shape)]
    longest = drawn.shape.index(max(drawn.shape))
    neighbour = place[:longest] + [(place[longest] + 1) % drawn.shape[longest]] + place[longest + 1:]
    return drawn.at[tuple(place)].set(least).at[tuple(neighbour)].set(top_value)


def strengthened(entries, own_key, source, target, shards_of, factor):
    owner, partner = [(jnp.arange(entries.shape[axis_at]) // (entries.shape[axis_at] // shards_of)).reshape([-1 if axis == axis_at else 1 for axis in range(entries.ndim)]) for axis_at in (source, target)]
    chosen = jax.random.permutation(own_key, shards_of)[partner]
    strong = (owner == chosen) | (owner == (partner + shards_of // 2) % shards_of)
    return jnp.where(strong, factor * entries, entries)


def block_levels(key, extent, pieces, least, largest):
    def one(dim, shards_of):
        heights = jax.random.uniform(jax.random.fold_in(jax.random.fold_in(key, 6), dim), (shards_of,), jnp.float32, least / len(pieces), largest / len(pieces))
        return jnp.repeat(jnp.exp(heights), extent[dim] // shards_of).reshape((-1,) + (1,) * (len(extent) - dim - 1))

    level = one(*pieces[0])
    for cut in pieces[1:]:
        level = level * one(*cut)
    return level


def split_up(count, total, bound, lean):
    loads = [(1 << 20) // math.isqrt(standing ** lean) + 1 for standing in range(2, count + 1)]
    spare, given = total - bound - (count - 1), [1] * (count - 1)
    while spare > 0:
        free = [i for i in range(count - 1) if given[i] < bound]
        mass, left = sum([loads[i] for i in free]), spare
        for i in free:
            more = min(bound - given[i], max(1, left * loads[i] // mass), spare)
            given[i] = given[i] + more
            spare = spare - more
    return np.array([bound] + given)


def uneven(rng, count, total, reach, skew):
    if count == 2:
        one = jax.random.randint(rng, (), max(1, total - reach), min(reach, total - 1) + 1)
        return jnp.stack([one, total - one])
    lengths = jnp.asarray(split_up(count, total, reach, skew), jnp.int32)
    couples = (count - 1) // 2
    source_of, receiver = lengths[1:1 + 2 * couples:2], lengths[2:2 + 2 * couples:2]
    slack = jnp.minimum(source_of - 1, reach - receiver)
    passed = jax.random.randint(jax.random.fold_in(rng, 1), (couples,), 0, 1 << 20) % (slack + 1)
    lengths = lengths.at[1:1 + 2 * couples:2].set(source_of - passed).at[2:2 + 2 * couples:2].set(receiver + passed)
    return lengths[jax.random.permutation(jax.random.fold_in(rng, 2), count)]


def scatter_about(key, extent, width, limit, cuts=(), kind=jnp.bfloat16):
    values = width * jax.random.normal(key, extent, jnp.float32)
    if cuts:
        values = values * block_levels(key, extent, cuts, -0.22, 0.18)
    return jnp.clip(values, -limit, limit).astype(kind)


def bell_draw_with(key, dims, deviation, reach, pieces, heavy, held_as=jnp.bfloat16):
    entries = deviation * jax.random.normal(key, dims, jnp.float32)
    if pieces:
        entries = entries * block_levels(key, dims, pieces, -0.22, 0.18)
    return jnp.clip(strengthened(entries, jax.random.fold_in(key, 3), *heavy), -reach, reach).astype(held_as)


def setup_inputs(seed: int = 0, part: int = 0) -> dict:
    splits = jax.random.split(jax.random.key(seed), 9)
    own_keys = jax.random.split(jax.random.fold_in(splits[8], part), 9)
    return {
        "layer_in": scatter_about(own_keys[0], (TOKENS, D), 1.0, 6.0, ((0, 16),)),
        "grad_out": scatter_about(own_keys[1], (TOKENS, D), 1.0, 6.0, ((0, 16),)),
        "in_proj": scatter_about(splits[2], (D, R), D ** -0.5, 0.125),
        "out_proj": scatter_about(splits[3], (D, R), D ** -0.5, 0.125),
        "queries": bell_draw_with(own_keys[4], (QUERIES, FEATS), (FEATS * SEQ_LEN) ** -0.5, 0.00390625, ((0, 4), (1, 4)), (1, 0, 4, 2.0)),
        "seq_ids": jax.vmap(lambda own: jnp.searchsorted(jnp.cumsum(uneven(own, SEQ_DEV, TOK_DEV, WIN, 0)), jnp.arange(TOK_DEV), side="right"))(jax.random.split(own_keys[5], GROUPS)).reshape((GROUPS, TOK_DEV)).astype(jnp.int32),
        "valid_counts": plant(jax.random.randint(own_keys[6], (SEQUENCES,), WIN // 8, WIN + 1), jax.random.fold_in(own_keys[6], 1), WIN // 8, WIN).astype(jnp.int32),
        "owner_order": draw_owner_order(jax.random.fold_in(jax.random.fold_in(splits[8], part), 71), part),
    }


def sequence_grads(in_low, out_low, labels, counts):
    member = (labels[:, None] == jnp.arange(SEQ_DEV, dtype=jnp.int32)[None, :]).astype(jnp.int32)
    seg_len = jnp.sum(member, axis=0).astype(jnp.int32)
    starts = (jnp.cumsum(seg_len) - seg_len).astype(jnp.int32)
    position = jnp.arange(TOK_DEV, dtype=jnp.int32) - starts[labels]
    counted = (position < counts[labels]).astype(jnp.float32)
    weighted = in_low.astype(jnp.float32) * counted[:, None]
    member_f = member.astype(jnp.float32)
    grads = jnp.einsum("ts,ti,tj->sij", member_f, weighted, out_low.astype(jnp.float32), precision=lax.Precision.HIGHEST)
    return grads.reshape(SEQ_DEV, R * R).astype(jnp.bfloat16)


def reference(layer_in, grad_out, in_proj, out_proj, queries, seq_ids, valid_counts, owner_order):
    layer_blocks = layer_in.reshape(GROUPS, TOK_DEV, D)
    grad_blocks = grad_out.reshape(GROUPS, TOK_DEV, D)
    count_blocks = valid_counts.reshape(GROUPS, SEQ_DEV)

    def one_block(inputs):
        layer_rows, grad_rows, labels, counts = inputs
        in_low = jnp.dot(layer_rows, in_proj, preferred_element_type=jnp.float32).astype(jnp.bfloat16)
        out_low = jnp.dot(grad_rows, out_proj, preferred_element_type=jnp.float32).astype(jnp.bfloat16)
        return sequence_grads(in_low, out_low, labels, counts)

    seq_grads = lax.map(one_block, (layer_blocks, grad_blocks, seq_ids, count_blocks))
    seq_grads = seq_grads.reshape(SEQUENCES, R * R)
    score = lax.dot_general(queries, seq_grads, (((1,), (1,)), ((), ())), preferred_element_type=jnp.float32)
    return jnp.take(score, owner_order, axis=0)
```

```python
import functools

import jax
import jax.numpy as jnp
from jax import lax
from jax.experimental import pallas as pl
from jax.experimental.pallas import tpu as pltpu
from jax.sharding import PartitionSpec as P

MESH = pl.DeviceIdType.MESH
F32 = jnp.float32
BF16 = jnp.bfloat16
VMEM = 67043328
LAG = 3


def flip(i, m):
    bit = 1
    while bit <= m:
        if m & bit:
            i = i + bit - 2 * bit * (lax.div(i, bit) % 2)
        bit *= 2
    return i


def bits_of(n):
    got = []
    bit = n // 2
    while bit >= 1:
        got.append(bit)
        bit //= 2
    return got


def kernel(fn, dn, chunks, tiles, lag, fold, relay, x_hbm, g_hbm, wi_hbm, wo_hbm, q_hbm, ids, cnt, order, out,
           x_buf, g_buf, wi, wo, q_buf, in_t, out_low, mask, sent, far_out, far_in, far_mask, held, acc, perm, piece,
           landed, w_sem, x_sem, g_sem, q_sem, a_send, a_recv, f_send, f_recv, d_send, d_recv, r_send, r_recv):
    me_f = lax.axis_index("feat")
    me_d = lax.axis_index("dp")
    slab, seqs, width = held.shape[2:]
    tokens = x_buf.shape[0]
    tile = tokens // tiles
    q_rows, feats = q_buf.shape
    rows = q_rows // fn
    part = slab // chunks
    cols = dn * seqs
    bits = bits_of(dn)
    last = len(bits)
    mate = flip(me_f, 1)
    upper = lax.div(me_f, 2)
    inner = lax.rem(me_f + 1, 4) >= 2
    gateway = 2 - upper

    w_copies = [
        pltpu.make_async_copy(wi_hbm, wi, w_sem.at[0]),
        pltpu.make_async_copy(wo_hbm, wo, w_sem.at[1]),
    ]
    x_copies = []
    g_copies = []
    for t in range(tiles):
        at = pl.ds(t * tile, tile)
        x_copies.append(pltpu.make_async_copy(x_hbm.at[at], x_buf.at[at], x_sem.at[t]))
        g_copies.append(pltpu.make_async_copy(g_hbm.at[at], g_buf.at[at], g_sem.at[t]))
    w_copies[0].start()
    x_copies[0].start()
    w_copies[1].start()
    g_copies[0].start()
    for t in range(1, tiles):
        x_copies[t].start()
        g_copies[t].start()
    q_copy = pltpu.make_async_copy(q_hbm, q_buf, q_sem)

    barrier = pltpu.get_barrier_semaphore()
    for r in range(1, fn):
        pl.semaphore_signal(barrier, inc=1, device_id={"feat": flip(me_f, r)}, device_id_type=MESH)
    for b in bits:
        pl.semaphore_signal(barrier, inc=1, device_id={"dp": flip(me_d, b)}, device_id_type=MESH)

    labels = ids[...]
    seq = lax.broadcasted_iota(jnp.int32, (seqs, tokens), 0)
    place = lax.broadcasted_iota(jnp.int32, (seqs, tokens), 1)
    starts = jnp.sum((labels < seq).astype(F32), axis=1, keepdims=True).astype(jnp.int32)
    one_r = lax.broadcasted_iota(jnp.int32, (seqs, seqs), 0)
    one_c = lax.broadcasted_iota(jnp.int32, (seqs, seqs), 1)
    counts = jnp.where(one_r == one_c, cnt[...].astype(F32), 0.0)
    counts = jnp.sum(counts, axis=1, keepdims=True).astype(jnp.int32)
    mask[...] = ((labels == seq) & (place - starts < counts)).astype(BF16)
    at_row = lax.broadcasted_iota(jnp.int32, (q_rows, q_rows), 0)
    perm[...] = ((order[...] % q_rows) == at_row).astype(F32).T.astype(BF16)

    def source(k):
        if not relay or k < 2:
            return flip(me_f, ranks[k])
        return gateway if k == 2 else 3 * (1 - upper)

    if relay:
        ranks = [0, 1]
    else:
        ranks = sorted(range(fn), key=lambda r: (bin(r).count("1"), r))

    def far(kind, i, which=0):
        slot = jnp.where(inner, 0, 1)
        if kind == "out":
            at = pl.ds(i * tile, tile)
            src, dst, sem = out_low.at[at], far_out.at[slot, at], i
        elif kind == "mask":
            src, dst, sem = mask, far_mask.at[slot], tiles
        else:
            want = gateway if which == 0 else flip(gateway, 1)
            row = pl.multiple_of(want * slab + i * part, part)
            src, dst = in_t.at[pl.ds(row, part)], far_in.at[slot, which, pl.ds(i * part, part)]
            sem = tiles + 1 + 2 * i + which
        return pltpu.make_async_remote_copy(
            src_ref=src,
            dst_ref=dst,
            send_sem=f_send.at[sem],
            recv_sem=f_recv.at[slot, sem],
            device_id={"feat": gateway},
            device_id_type=MESH,
        )

    def far_wait(slot, sem, ref):
        pltpu.make_async_copy(ref, ref, f_recv.at[slot, sem]).wait()

    for t in range(tiles):
        at = slice(t * tile, (t + 1) * tile)
        if t == 0:
            w_copies[0].wait()
        x_copies[t].wait()
        low = jnp.dot(x_buf[at, :], wi[...], preferred_element_type=F32)
        in_t[:, at] = low.T.astype(BF16)
        if t == 0:
            w_copies[1].wait()
        g_copies[t].wait()
        out_low[at, :] = jnp.dot(g_buf[at, :], wo[...], preferred_element_type=F32).astype(BF16)
        if t == 0:
            pl.semaphore_wait(barrier, fn - 1 + last)
        if relay:
            @pl.when(inner)
            def _():
                if t == 0:
                    far("mask", 0).start()
                far("out", t).start()
    q_copy.start()

    def grads(lows, masks, outs):
        left = lows.astype(F32)[:, None, :] * masks.astype(F32)[None, :, :]
        left = left.reshape(part * seqs, tokens).astype(BF16)
        got = jnp.dot(left, outs, preferred_element_type=F32)
        return got.astype(BF16).reshape(part, seqs, width)

    def mine(index, c):
        row = pl.multiple_of(index * slab + c * part, 8)
        return grads(in_t[pl.ds(row, part), :], mask[...], out_low[...])

    def across(k, c):
        span = pl.ds(c * part, part)
        block = source(k) if relay and k > 1 else me_f
        return pltpu.make_async_remote_copy(
            src_ref=sent.at[k - 1, span],
            dst_ref=held.at[block, me_d, span],
            send_sem=a_send.at[k, c],
            recv_sem=a_recv.at[k, c],
            device_id={"feat": mate if relay else source(k)},
            device_id_type=MESH,
        )

    def along(k, m, b, c):
        block = held.at[source(k), flip(me_d, m), pl.ds(c * part, part)]
        return pltpu.make_async_remote_copy(
            src_ref=block,
            dst_ref=block,
            send_sem=d_send.at[k, m + b, c],
            recv_sem=d_recv.at[k, m + b, c],
            device_id={"dp": flip(me_d, b)},
            device_id_type=MESH,
        )

    def masks_before(k):
        got = [0]
        for b in bits[:k]:
            got = got + [m + b for m in got]
        return got

    events = [(k, c) for k in range(fn) for c in range(chunks)]

    for c in range(chunks):
        span = pl.ds(c * part, part)
        held[me_f, me_d, span] = mine(me_f, c)
        for b in bits:
            along(0, 0, b, c).start()
        for k in range(1, 2 if relay else fn):
            sent[k - 1, span] = mine(source(k), c)
            across(k, c).start()
        if relay:
            @pl.when(inner)
            def _():
                far("in", c, 0).start()
                far("in", c, 1).start()

    def arrive(k, c):
        span = pl.ds(c * part, part)
        if k == 0:
            return
        if not relay or k == 1:
            across(k, c).wait_recv()
            if relay and c == chunks - 1:
                @pl.when(jnp.logical_not(inner))
                def _():
                    far("mask", 0).start()
                    for t in range(tiles):
                        far("out", t).start()
                    for i in range(chunks):
                        far("in", i, 0).start()
                        far("in", i, 1).start()
            return
        slot = k - 2

        @pl.when(inner)
        def _():
            if c == 0:
                far_wait(slot, tiles, far_mask.at[slot])
                for t in range(tiles):
                    far_wait(slot, t, far_out.at[slot, pl.ds(t * tile, tile)])
            for which in (1, 0):
                far_wait(slot, tiles + 1 + 2 * c + which, far_in.at[slot, which, span])
            sent[k - 1, span] = grads(far_in[slot, 1, span], far_mask[slot], far_out[slot])
            across(k, c).start()
            held[source(k), me_d, span] = grads(far_in[slot, 0, span], far_mask[slot], far_out[slot])

        @pl.when(jnp.logical_not(inner))
        def _():
            across(k, c).wait_recv()

    def stage(n, k, c):
        if n == 0:
            arrive(k, c)
        else:
            for m in masks_before(n - 1):
                along(k, m, bits[n - 1], c).wait_recv()
        if n < last:
            for m in masks_before(n):
                if k > 0 or m > 0:
                    along(k, m, bits[n], c).start()

    def share(t, k):
        other = flip(me_f, t)
        return pltpu.make_async_remote_copy(
            src_ref=piece.at[k, other],
            dst_ref=landed.at[t, source(k)],
            send_sem=r_send.at[t, k],
            recv_sem=r_recv.at[t, k],
            device_id={"feat": other},
            device_id_type=MESH,
        )

    def score(k, c):
        blocks = [held[source(k), :, c * part + i].reshape(cols, width) for i in range(part)]
        span = slice(c * part * width, (c + 1) * part * width)
        got = lax.dot_general(
            q_buf[:, span], jnp.concatenate(blocks, axis=1), (((1,), (1,)), ((), ())), preferred_element_type=F32
        )
        if c > 0:
            got = acc[...] + got
        if c < chunks - 1:
            acc[...] = got
            return
        short = rows // fold
        for d in range(fn):
            cut = [got[d * rows + i * short:d * rows + (i + 1) * short] for i in range(fold)]
            piece[k, d] = jnp.concatenate(cut, axis=1)
        for t in range(1, fn):
            share(t, k).start()
        landed[0, source(k)] = piece[k, me_f]

    def assemble(s):
        short = rows // fold
        total = landed[0, s]
        for t in range(1, fn):
            total = total + landed[t, s]
        for i in range(fold):
            for m in range(dn):
                at = (m * fn + s) * seqs
                out[i * short:(i + 1) * short, at:at + seqs] = total[:, i * cols + m * seqs:i * cols + (m + 1) * seqs]

    lags = [0] + [lag + n for n in range(last)]
    steps = len(events) + lags[-1]
    wide = min(feats, 1024)
    for e in range(steps):
        if e == lags[-1]:
            q_copy.wait()

            def reorder(i, carry):
                at = pl.ds(pl.multiple_of(i * wide, wide), wide)
                q_buf[:, at] = jnp.dot(perm[...], q_buf[:, at], preferred_element_type=F32).astype(BF16)
                return carry

            lax.fori_loop(0, feats // wide, reorder, 0)
        if relay and e == steps - 1:
            for k in range(fn - 1):
                for t in range(1, fn):
                    share(t, k).wait_recv()
            for s in (1, 2):
                assemble(s)
        for n in range(last + 1):
            if 0 <= e - lags[n] < len(events):
                stage(n, *events[e - lags[n]])
        if e >= lags[-1]:
            score(*events[e - lags[-1]])

    for k in range(fn - 1 if relay else 0, fn):
        for t in range(1, fn):
            share(t, k).wait_recv()
    for s in (0, 3) if relay else range(fn):
        assemble(s)

    for k in range(fn):
        for t in range(1, fn):
            share(t, k).wait_send()
    for k in range(1, 2 if relay else fn):
        for c in range(chunks):
            across(k, c).wait_send()
    if relay:
        @pl.when(inner)
        def _():
            for k in range(2, fn):
                for c in range(chunks):
                    across(k, c).wait_send()

        far("mask", 0).wait_send()
        for t in range(tiles):
            far("out", t).wait_send()
        for c in range(chunks):
            far("in", c, 0).wait_send()
            far("in", c, 1).wait_send()
    for k, c in events:
        for n, b in enumerate(bits):
            for m in masks_before(n):
                along(k, m, b, c).wait_send()


def local(fn, dn, layer_in, grad_out, in_proj, out_proj, queries, seq_ids, valid_counts, owner_order):
    tokens, model = layer_in.shape
    width = in_proj.shape[1]
    seqs = valid_counts.shape[0]
    q_rows, feats = queries.shape
    slab = width // fn
    rows = q_rows // fn
    chunks = max(1, min(4, slab // 16))
    tiles = max(1, min(4, tokens // 256))
    relay = fn == 4 and slab % 16 == 0
    fold = 2 if dn * seqs == 64 and rows % 16 == 0 else 1
    slots = 2 if relay else 1
    far_rows = slab if relay else 16
    dma = pltpu.SemaphoreType.DMA
    hbm = pl.BlockSpec(memory_space=pl.ANY)
    vmem = pl.BlockSpec(memory_space=pltpu.VMEM)
    return pl.pallas_call(
        functools.partial(kernel, fn, dn, chunks, tiles, LAG, fold, relay),
        out_shape=jax.ShapeDtypeStruct((rows, dn * fn * seqs), F32),
        in_specs=[hbm] * 5 + [vmem] * 3,
        out_specs=vmem,
        scratch_shapes=[
            pltpu.VMEM((tokens, model), BF16),
            pltpu.VMEM((tokens, model), BF16),
            pltpu.VMEM((model, width), BF16),
            pltpu.VMEM((model, width), BF16),
            pltpu.VMEM((q_rows, feats), BF16),
            pltpu.VMEM((width, tokens), BF16),
            pltpu.VMEM((tokens, width), BF16),
            pltpu.VMEM((seqs, tokens), BF16),
            pltpu.VMEM((fn - 1, slab, seqs, width), BF16),
            pltpu.VMEM((slots, tokens, width), BF16),
            pltpu.VMEM((slots, 2, far_rows, tokens), BF16),
            pltpu.VMEM((slots, seqs, tokens), BF16),
            pltpu.VMEM((fn, dn, slab, seqs, width), BF16),
            pltpu.VMEM((q_rows, dn * seqs), F32),
            pltpu.VMEM((q_rows, q_rows), BF16),
            pltpu.VMEM((fn, fn, rows // fold, fold * dn * seqs), F32),
            pltpu.VMEM((fn, fn, rows // fold, fold * dn * seqs), F32),
            dma((2,)),
            dma((tiles,)),
            dma((tiles,)),
            dma,
            dma((fn, chunks)),
            dma((fn, chunks)),
            dma((tiles + 1 + 2 * chunks,)),
            dma((slots, tiles + 1 + 2 * chunks)),
            dma((fn, dn, chunks)),
            dma((fn, dn, chunks)),
            dma((fn, fn)),
            dma((fn, fn)),
        ],
        compiler_params=pltpu.CompilerParams(
            collective_id=0, has_side_effects=True, vmem_limit_bytes=VMEM
        ),
    )(layer_in, grad_out, in_proj, out_proj, queries, seq_ids, valid_counts.reshape(1, seqs), owner_order.reshape(1, q_rows))


def solution(mesh):
    in_specs = (
        P(("dom", "dp", "feat"), None),
        P(("dom", "dp", "feat"), None),
        P(),
        P(),
        P(("dom", "dp"), "feat"),
        P(("dom", "dp", "feat"), None),
        P(("dom", "dp", "feat")),
        P(("dom", "dp")),
    )
    out_specs = P(("dom", "dp", "feat"), None)
    body = functools.partial(local, mesh.shape["feat"], mesh.shape["dp"])
    return jax.shard_map(body, mesh=mesh, in_specs=in_specs, out_specs=out_specs, check_vma=False)
```

```python
import functools

import jax
import jax.numpy as jnp
from jax import lax
from jax.experimental import pallas as pl
from jax.experimental.pallas import tpu as pltpu
from jax.sharding import PartitionSpec as P

MESH = pl.DeviceIdType.MESH
F32 = jnp.float32
BF16 = jnp.bfloat16
VMEM = 67043328
LAG = 3
PIECES = 4


def flip(i, m):
    bit = 1
    while bit <= m:
        if m & bit:
            i = i + bit - 2 * bit * (lax.div(i, bit) % 2)
        bit *= 2
    return i


def bits_of(n):
    got = []
    bit = n // 2
    while bit >= 1:
        got.append(bit)
        bit //= 2
    return got


def kernel(fn, dn, chunks, tiles, pieces, lag, fold, relay, x_hbm, g_hbm, wi_hbm, wo_hbm, q_hbm, ids, cnt, order, out,
           x_buf, g_buf, wi, wo, q_buf, in_t, out_low, mask, sent, far_out, far_in, far_mask, held, acc, perm, piece,
           landed, w_sem, x_sem, g_sem, q_sem, a_send, a_recv, f_send, f_recv, d_send, d_recv, r_send, r_recv, go):
    me_f = lax.axis_index("feat")
    me_d = lax.axis_index("dp")
    slab, seqs, width = held.shape[2:]
    tokens = x_buf.shape[0]
    tile = tokens // tiles
    bit_of = tokens // pieces
    q_rows, feats = q_buf.shape
    rows = q_rows // fn
    part = slab // chunks
    cols = dn * seqs
    bits = bits_of(dn)
    last = len(bits)
    mate = flip(me_f, 1)
    upper = lax.div(me_f, 2)
    inner = lax.rem(me_f + 1, 4) >= 2
    gateway = 2 - upper

    w_copies = [
        pltpu.make_async_copy(wi_hbm, wi, w_sem.at[0]),
        pltpu.make_async_copy(wo_hbm, wo, w_sem.at[1]),
    ]
    x_copies = []
    g_copies = []
    for t in range(tiles):
        at = pl.ds(t * tile, tile)
        x_copies.append(pltpu.make_async_copy(x_hbm.at[at], x_buf.at[at], x_sem.at[t]))
        g_copies.append(pltpu.make_async_copy(g_hbm.at[at], g_buf.at[at], g_sem.at[t]))
    w_copies[0].start()
    x_copies[0].start()
    w_copies[1].start()
    g_copies[0].start()
    for t in range(1, tiles):
        x_copies[t].start()
        g_copies[t].start()
    q_copy = pltpu.make_async_copy(q_hbm, q_buf, q_sem)

    barrier = pltpu.get_barrier_semaphore()
    for r in range(1, fn):
        pl.semaphore_signal(barrier, inc=1, device_id={"feat": flip(me_f, r)}, device_id_type=MESH)
    for b in bits:
        pl.semaphore_signal(barrier, inc=1, device_id={"dp": flip(me_d, b)}, device_id_type=MESH)

    labels = ids[...]
    seq = lax.broadcasted_iota(jnp.int32, (seqs, tokens), 0)
    place = lax.broadcasted_iota(jnp.int32, (seqs, tokens), 1)
    starts = jnp.sum((labels < seq).astype(F32), axis=1, keepdims=True).astype(jnp.int32)
    one_r = lax.broadcasted_iota(jnp.int32, (seqs, seqs), 0)
    one_c = lax.broadcasted_iota(jnp.int32, (seqs, seqs), 1)
    counts = jnp.where(one_r == one_c, cnt[...].astype(F32), 0.0)
    counts = jnp.sum(counts, axis=1, keepdims=True).astype(jnp.int32)
    mask[...] = ((labels == seq) & (place - starts < counts)).astype(BF16)
    at_row = lax.broadcasted_iota(jnp.int32, (q_rows, q_rows), 0)
    perm[...] = ((order[...] % q_rows) == at_row).astype(F32).T.astype(BF16)

    def source(k):
        if not relay or k < 2:
            return flip(me_f, ranks[k])
        return gateway if k == 2 else 3 * (1 - upper)

    if relay:
        ranks = [0, 1]
    else:
        ranks = sorted(range(fn), key=lambda r: (bin(r).count("1"), r))

    def far(kind, i, which=0):
        slot = jnp.where(inner, 0, 1)
        if kind == "out":
            at = pl.ds(i * bit_of, bit_of)
            src, dst, sem = out_low.at[at], far_out.at[slot, at], i
        elif kind == "mask":
            src, dst, sem = mask, far_mask.at[slot], pieces
        else:
            want = gateway if which == 0 else flip(gateway, 1)
            row = pl.multiple_of(want * slab + i * part, part)
            src, dst = in_t.at[pl.ds(row, part)], far_in.at[slot, which, pl.ds(i * part, part)]
            sem = pieces + 1 + 2 * i + which
        return pltpu.make_async_remote_copy(
            src_ref=src,
            dst_ref=dst,
            send_sem=f_send.at[sem],
            recv_sem=f_recv.at[slot, sem],
            device_id={"feat": gateway},
            device_id_type=MESH,
        )

    def far_wait(slot, sem, ref):
        pltpu.make_async_copy(ref, ref, f_recv.at[slot, sem]).wait()

    for t in range(tiles):
        at = slice(t * tile, (t + 1) * tile)
        if t == 0:
            w_copies[0].wait()
        x_copies[t].wait()
        low = jnp.dot(x_buf[at, :], wi[...], preferred_element_type=F32)
        in_t[:, at] = low.T.astype(BF16)
        if t == 0:
            w_copies[1].wait()
        g_copies[t].wait()
        out_low[at, :] = jnp.dot(g_buf[at, :], wo[...], preferred_element_type=F32).astype(BF16)
        if t == 0:
            pl.semaphore_wait(barrier, fn - 1 + last)
        if relay:
            @pl.when(inner)
            def _():
                if t == 0:
                    far("mask", 0).start()
                for i in range(t * pieces // tiles, (t + 1) * pieces // tiles):
                    far("out", i).start()
    q_copy.start()

    def grads(lows, masks, outs):
        left = lows.astype(F32)[:, None, :] * masks.astype(F32)[None, :, :]
        left = left.reshape(part * seqs, tokens).astype(BF16)
        got = jnp.dot(left, outs, preferred_element_type=F32)
        return got.astype(BF16).reshape(part, seqs, width)

    def mine(index, c):
        row = pl.multiple_of(index * slab + c * part, 8)
        return grads(in_t[pl.ds(row, part), :], mask[...], out_low[...])

    def across(k, c):
        span = pl.ds(c * part, part)
        block = source(k) if relay and k > 1 else me_f
        return pltpu.make_async_remote_copy(
            src_ref=sent.at[k - 1, span],
            dst_ref=held.at[block, me_d, span],
            send_sem=a_send.at[k, c],
            recv_sem=a_recv.at[k, c],
            device_id={"feat": mate if relay else source(k)},
            device_id_type=MESH,
        )

    def along(k, m, b, c):
        block = held.at[source(k), flip(me_d, m), pl.ds(c * part, part)]
        return pltpu.make_async_remote_copy(
            src_ref=block,
            dst_ref=block,
            send_sem=d_send.at[k, m + b, c],
            recv_sem=d_recv.at[k, m + b, c],
            device_id={"dp": flip(me_d, b)},
            device_id_type=MESH,
        )

    def masks_before(k):
        got = [0]
        for b in bits[:k]:
            got = got + [m + b for m in got]
        return got

    events = [(k, c) for k in range(fn) for c in range(chunks)]

    for c in range(chunks):
        span = pl.ds(c * part, part)
        held[me_f, me_d, span] = mine(me_f, c)
        for b in bits:
            along(0, 0, b, c).start()
        for k in range(1, 2 if relay else fn):
            sent[k - 1, span] = mine(source(k), c)
            across(k, c).start()
        if relay:
            @pl.when(inner)
            def _():
                far("in", c, 0).start()
                far("in", c, 1).start()

    def arrive(k, c):
        span = pl.ds(c * part, part)
        if k == 0:
            return
        if not relay or k == 1:
            across(k, c).wait_recv()
            return
        slot = k - 2

        @pl.when(inner)
        def _():
            if c == 0:
                far_wait(slot, pieces, far_mask.at[slot])
                for t in range(pieces):
                    far_wait(slot, t, far_out.at[slot, pl.ds(t * bit_of, bit_of)])
            for which in (1, 0):
                far_wait(slot, pieces + 1 + 2 * c + which, far_in.at[slot, which, span])
            sent[k - 1, span] = grads(far_in[slot, 1, span], far_mask[slot], far_out[slot])
            across(k, c).start()
            held[source(k), me_d, span] = grads(far_in[slot, 0, span], far_mask[slot], far_out[slot])

        @pl.when(jnp.logical_not(inner))
        def _():
            across(k, c).wait_recv()

    def far_sent():
        far("mask", 0).wait_send()
        for t in range(pieces):
            far("out", t).wait_send()
        for i in range(chunks):
            far("in", i, 0).wait_send()
            far("in", i, 1).wait_send()

    def stage(n, k, c):
        if n == 0:
            arrive(k, c)
        else:
            for m in masks_before(n - 1):
                along(k, m, bits[n - 1], c).wait_recv()
        if n < last:
            for m in masks_before(n):
                if k > 0 or m > 0:
                    along(k, m, bits[n], c).start()
        if relay and n == 0 and (k, c) == (1, chunks - 1):
            @pl.when(inner)
            def _():
                far_sent()
                pl.semaphore_signal(go, inc=1, device_id={"feat": mate}, device_id_type=MESH)

            @pl.when(jnp.logical_not(inner))
            def _():
                pl.semaphore_wait(go, 1)
                far("mask", 0).start()
                for t in range(pieces):
                    far("out", t).start()
                for i in range(chunks):
                    far("in", i, 0).start()
                    far("in", i, 1).start()

    def share(t, k):
        other = flip(me_f, t)
        return pltpu.make_async_remote_copy(
            src_ref=piece.at[k, other],
            dst_ref=landed.at[t, source(k)],
            send_sem=r_send.at[t, k],
            recv_sem=r_recv.at[t, k],
            device_id={"feat": other},
            device_id_type=MESH,
        )

    def score(k, c):
        blocks = [held[source(k), :, c * part + i].reshape(cols, width) for i in range(part)]
        span = slice(c * part * width, (c + 1) * part * width)
        got = lax.dot_general(
            q_buf[:, span], jnp.concatenate(blocks, axis=1), (((1,), (1,)), ((), ())), preferred_element_type=F32
        )
        if c > 0:
            got = acc[...] + got
        if c < chunks - 1:
            acc[...] = got
            return
        short = rows // fold
        for d in range(fn):
            cut = [got[d * rows + i * short:d * rows + (i + 1) * short] for i in range(fold)]
            piece[k, d] = jnp.concatenate(cut, axis=1).astype(piece.dtype)
        for t in range(1, fn):
            share(t, k).start()
        landed[0, source(k)] = piece[k, me_f]

    def assemble(s):
        short = rows // fold
        total = landed[0, s].astype(F32)
        for t in range(1, fn):
            total = total + landed[t, s].astype(F32)
        for i in range(fold):
            for m in range(dn):
                at = (m * fn + s) * seqs
                out[i * short:(i + 1) * short, at:at + seqs] = total[:, i * cols + m * seqs:i * cols + (m + 1) * seqs]

    lags = [0] + [lag + n for n in range(last)]
    steps = len(events) + lags[-1]
    wide = min(feats, 1024)
    for e in range(steps):
        if e == lags[-1]:
            q_copy.wait()

            def reorder(i, carry):
                at = pl.ds(pl.multiple_of(i * wide, wide), wide)
                q_buf[:, at] = jnp.dot(perm[...], q_buf[:, at], preferred_element_type=F32).astype(BF16)
                return carry

            lax.fori_loop(0, feats // wide, reorder, 0)
        if relay and e == steps - 1:
            for k in range(fn - 1):
                for t in range(1, fn):
                    share(t, k).wait_recv()
            for s in (1, 2):
                assemble(s)
        for n in range(last + 1):
            if 0 <= e - lags[n] < len(events):
                stage(n, *events[e - lags[n]])
        if e >= lags[-1]:
            score(*events[e - lags[-1]])

    for k in range(fn - 1 if relay else 0, fn):
        for t in range(1, fn):
            share(t, k).wait_recv()
    for s in (0, 3) if relay else range(fn):
        assemble(s)

    for k in range(fn):
        for t in range(1, fn):
            share(t, k).wait_send()
    for k in range(1, 2 if relay else fn):
        for c in range(chunks):
            across(k, c).wait_send()
    if relay:
        @pl.when(inner)
        def _():
            for k in range(2, fn):
                for c in range(chunks):
                    across(k, c).wait_send()

        @pl.when(jnp.logical_not(inner))
        def _():
            far_sent()

    for k, c in events:
        for n, b in enumerate(bits):
            for m in masks_before(n):
                along(k, m, b, c).wait_send()


def local(fn, dn, layer_in, grad_out, in_proj, out_proj, queries, seq_ids, valid_counts, owner_order):
    tokens, model = layer_in.shape
    width = in_proj.shape[1]
    seqs = valid_counts.shape[0]
    q_rows, feats = queries.shape
    slab = width // fn
    rows = q_rows // fn
    chunks = max(1, min(4, slab // 16))
    tiles = max(1, min(2, tokens // 256))
    pieces = min(PIECES, tokens // 16)
    relay = fn == 4 and slab % 16 == 0
    fold = 2 if dn * seqs == 64 and rows % 32 == 0 else 1
    slots = 2 if relay else 1
    far_rows = slab if relay else 16
    dma = pltpu.SemaphoreType.DMA
    hbm = pl.BlockSpec(memory_space=pl.ANY)
    vmem = pl.BlockSpec(memory_space=pltpu.VMEM)
    return pl.pallas_call(
        functools.partial(kernel, fn, dn, chunks, tiles, pieces, LAG, fold, relay),
        out_shape=jax.ShapeDtypeStruct((rows, dn * fn * seqs), F32),
        in_specs=[hbm] * 5 + [vmem] * 3,
        out_specs=vmem,
        scratch_shapes=[
            pltpu.VMEM((tokens, model), BF16),
            pltpu.VMEM((tokens, model), BF16),
            pltpu.VMEM((model, width), BF16),
            pltpu.VMEM((model, width), BF16),
            pltpu.VMEM((q_rows, feats), BF16),
            pltpu.VMEM((width, tokens), BF16),
            pltpu.VMEM((tokens, width), BF16),
            pltpu.VMEM((seqs, tokens), BF16),
            pltpu.VMEM((fn - 1, slab, seqs, width), BF16),
            pltpu.VMEM((slots, tokens, width), BF16),
            pltpu.VMEM((slots, 2, far_rows, tokens), BF16),
            pltpu.VMEM((slots, seqs, tokens), BF16),
            pltpu.VMEM((fn, dn, slab, seqs, width), BF16),
            pltpu.VMEM((q_rows, dn * seqs), F32),
            pltpu.VMEM((q_rows, q_rows), BF16),
            pltpu.VMEM((fn, fn, rows // fold, fold * dn * seqs), BF16),
            pltpu.VMEM((fn, fn, rows // fold, fold * dn * seqs), BF16),
            dma((2,)),
            dma((tiles,)),
            dma((tiles,)),
            dma,
            dma((fn, chunks)),
            dma((fn, chunks)),
            dma((pieces + 1 + 2 * chunks,)),
            dma((slots, pieces + 1 + 2 * chunks)),
            dma((fn, dn, chunks)),
            dma((fn, dn, chunks)),
            dma((fn, fn)),
            dma((fn, fn)),
            pltpu.SemaphoreType.REGULAR,
        ],
        compiler_params=pltpu.CompilerParams(
            collective_id=0, has_side_effects=True, vmem_limit_bytes=VMEM
        ),
    )(layer_in, grad_out, in_proj, out_proj, queries, seq_ids, valid_counts.reshape(1, seqs), owner_order.reshape(1, q_rows))


def solution(mesh):
    in_specs = (
        P(("dom", "dp", "feat"), None),
        P(("dom", "dp", "feat"), None),
        P(),
        P(),
        P(("dom", "dp"), "feat"),
        P(("dom", "dp", "feat"), None),
        P(("dom", "dp", "feat")),
        P(("dom", "dp")),
    )
    out_specs = P(("dom", "dp", "feat"), None)
    body = functools.partial(local, mesh.shape["feat"], mesh.shape["dp"])
    return jax.shard_map(body, mesh=mesh, in_specs=in_specs, out_specs=out_specs, check_vma=False)
```

```python
import functools

import jax
import jax.numpy as jnp
from jax import lax
from jax.experimental import pallas as pl
from jax.experimental.pallas import tpu as pltpu
from jax.sharding import PartitionSpec as P

MESH = pl.DeviceIdType.MESH
F32 = jnp.float32
BF16 = jnp.bfloat16
VMEM = 67043328
LAG = 3
PIECES = 4


def flip(i, m):
    bit = 1
    while bit <= m:
        if m & bit:
            i = i + bit - 2 * bit * (lax.div(i, bit) % 2)
        bit *= 2
    return i


def bits_of(n):
    got = []
    bit = n // 2
    while bit >= 1:
        got.append(bit)
        bit //= 2
    return got


def kernel(fn, dn, chunks, tiles, pieces, lag, fold, relay, x_hbm, g_hbm, wi_hbm, wo_hbm, q_hbm, ids, cnt, order, out,
           x_buf, g_buf, wi, wo, q_buf, in_t, out_low, mask, sent, far_out, far_in, far_mask, held, acc, perm, piece,
           landed, w_sem, x_sem, g_sem, q_sem, a_send, a_recv, f_send, f_recv, d_send, d_recv, r_send, r_recv, go):
    me_f = lax.axis_index("feat")
    me_d = lax.axis_index("dp")
    slab, seqs, width = held.shape[2:]
    tokens = x_buf.shape[0]
    tile = tokens // tiles
    bit_of = tokens // pieces
    q_rows, feats = q_buf.shape
    rows = q_rows // fn
    part = slab // chunks
    cols = dn * seqs
    bits = bits_of(dn)
    last = len(bits)
    mate = flip(me_f, 1)
    upper = lax.div(me_f, 2)
    inner = lax.rem(me_f + 1, 4) >= 2
    gateway = 2 - upper

    w_copies = [
        pltpu.make_async_copy(wi_hbm, wi, w_sem.at[0]),
        pltpu.make_async_copy(wo_hbm, wo, w_sem.at[1]),
    ]
    x_copies = []
    g_copies = []
    for t in range(tiles):
        at = pl.ds(t * tile, tile)
        x_copies.append(pltpu.make_async_copy(x_hbm.at[at], x_buf.at[at], x_sem.at[t]))
        g_copies.append(pltpu.make_async_copy(g_hbm.at[at], g_buf.at[at], g_sem.at[t]))
    w_copies[0].start()
    x_copies[0].start()
    w_copies[1].start()
    g_copies[0].start()
    for t in range(1, tiles):
        x_copies[t].start()
        g_copies[t].start()
    q_copy = pltpu.make_async_copy(q_hbm, q_buf, q_sem)

    barrier = pltpu.get_barrier_semaphore()
    for r in range(1, fn):
        pl.semaphore_signal(barrier, inc=1, device_id={"feat": flip(me_f, r)}, device_id_type=MESH)
    for b in bits:
        pl.semaphore_signal(barrier, inc=1, device_id={"dp": flip(me_d, b)}, device_id_type=MESH)

    labels = ids[...]
    seq = lax.broadcasted_iota(jnp.int32, (seqs, tokens), 0)
    place = lax.broadcasted_iota(jnp.int32, (seqs, tokens), 1)
    starts = jnp.sum((labels < seq).astype(F32), axis=1, keepdims=True).astype(jnp.int32)
    one_r = lax.broadcasted_iota(jnp.int32, (seqs, seqs), 0)
    one_c = lax.broadcasted_iota(jnp.int32, (seqs, seqs), 1)
    counts = jnp.where(one_r == one_c, cnt[...].astype(F32), 0.0)
    counts = jnp.sum(counts, axis=1, keepdims=True).astype(jnp.int32)
    mask[...] = ((labels == seq) & (place - starts < counts)).astype(BF16)
    at_row = lax.broadcasted_iota(jnp.int32, (q_rows, q_rows), 0)
    perm[...] = ((order[...] % q_rows) == at_row).astype(F32).T.astype(BF16)

    def source(k):
        if not relay or k < 2:
            return flip(me_f, ranks[k])
        return gateway if k == 2 else 3 * (1 - upper)

    if relay:
        ranks = [0, 1]
    else:
        ranks = sorted(range(fn), key=lambda r: (bin(r).count("1"), r))

    def far(kind, i, which=0):
        slot = jnp.where(inner, 0, 1)
        if kind == "out":
            at = pl.ds(i * bit_of, bit_of)
            src, dst, sem = out_low.at[at], far_out.at[slot, at], i
        elif kind == "mask":
            src, dst, sem = mask, far_mask.at[slot], pieces
        else:
            want = gateway if which == 0 else flip(gateway, 1)
            row = pl.multiple_of(want * slab + i * part, part)
            src, dst = in_t.at[pl.ds(row, part)], far_in.at[slot, which, pl.ds(i * part, part)]
            sem = pieces + 1 + 2 * i + which
        return pltpu.make_async_remote_copy(
            src_ref=src,
            dst_ref=dst,
            send_sem=f_send.at[sem],
            recv_sem=f_recv.at[slot, sem],
            device_id={"feat": gateway},
            device_id_type=MESH,
        )

    def far_wait(slot, sem, ref):
        pltpu.make_async_copy(ref, ref, f_recv.at[slot, sem]).wait()

    for t in range(tiles):
        at = slice(t * tile, (t + 1) * tile)
        if t == 0:
            w_copies[0].wait()
        x_copies[t].wait()
        low = jnp.dot(x_buf[at, :], wi[...], preferred_element_type=F32)
        in_t[:, at] = low.T.astype(BF16)
        if t == 0:
            w_copies[1].wait()
        g_copies[t].wait()
        out_low[at, :] = jnp.dot(g_buf[at, :], wo[...], preferred_element_type=F32).astype(BF16)
        if t == 0:
            pl.semaphore_wait(barrier, fn - 1 + last)
        if relay:
            @pl.when(inner)
            def _():
                if t == 0:
                    far("mask", 0).start()
                for i in range(t * pieces // tiles, (t + 1) * pieces // tiles):
                    far("out", i).start()
    q_copy.start()

    def grads(lows, masks, outs):
        left = lows.astype(F32)[:, None, :] * masks.astype(F32)[None, :, :]
        left = left.reshape(part * seqs, tokens).astype(BF16)
        got = jnp.dot(left, outs, preferred_element_type=F32)
        return got.astype(BF16).reshape(part, seqs, width)

    def mine(index, c):
        row = pl.multiple_of(index * slab + c * part, 8)
        return grads(in_t[pl.ds(row, part), :], mask[...], out_low[...])

    def across(k, c):
        span = pl.ds(c * part, part)
        block = source(k) if relay and k > 1 else me_f
        return pltpu.make_async_remote_copy(
            src_ref=sent.at[k - 1, span],
            dst_ref=held.at[block, me_d, span],
            send_sem=a_send.at[k, c],
            recv_sem=a_recv.at[k, c],
            device_id={"feat": mate if relay else source(k)},
            device_id_type=MESH,
        )

    def along(k, m, b, c):
        block = held.at[source(k), flip(me_d, m), pl.ds(c * part, part)]
        return pltpu.make_async_remote_copy(
            src_ref=block,
            dst_ref=block,
            send_sem=d_send.at[k, m + b, c],
            recv_sem=d_recv.at[k, m + b, c],
            device_id={"dp": flip(me_d, b)},
            device_id_type=MESH,
        )

    def masks_before(k):
        got = [0]
        for b in bits[:k]:
            got = got + [m + b for m in got]
        return got

    events = [(k, c) for k in range(fn) for c in range(chunks)]

    for c in range(chunks):
        span = pl.ds(c * part, part)
        held[me_f, me_d, span] = mine(me_f, c)
        for b in bits:
            along(0, 0, b, c).start()
        for k in range(1, 2 if relay else fn):
            sent[k - 1, span] = mine(source(k), c)
            across(k, c).start()
        if relay:
            @pl.when(inner)
            def _():
                far("in", c, 0).start()
                far("in", c, 1).start()

    def arrive(k, c):
        span = pl.ds(c * part, part)
        if k == 0:
            return
        if not relay or k == 1:
            across(k, c).wait_recv()
            return
        slot = k - 2

        @pl.when(inner)
        def _():
            if c == 0:
                far_wait(slot, pieces, far_mask.at[slot])
                for t in range(pieces):
                    far_wait(slot, t, far_out.at[slot, pl.ds(t * bit_of, bit_of)])
            for which in (1, 0):
                far_wait(slot, pieces + 1 + 2 * c + which, far_in.at[slot, which, span])
            sent[k - 1, span] = grads(far_in[slot, 1, span], far_mask[slot], far_out[slot])
            across(k, c).start()
            held[source(k), me_d, span] = grads(far_in[slot, 0, span], far_mask[slot], far_out[slot])

        @pl.when(jnp.logical_not(inner))
        def _():
            across(k, c).wait_recv()

    def far_sent():
        far("mask", 0).wait_send()
        for t in range(pieces):
            far("out", t).wait_send()
        for i in range(chunks):
            far("in", i, 0).wait_send()
            far("in", i, 1).wait_send()

    def stage(n, k, c):
        if n == 0:
            arrive(k, c)
        else:
            for m in masks_before(n - 1):
                along(k, m, bits[n - 1], c).wait_recv()
        if n < last:
            for m in masks_before(n):
                if k > 0 or m > 0:
                    along(k, m, bits[n], c).start()
        if relay and n == 0 and (k, c) == (1, chunks - 1):
            @pl.when(inner)
            def _():
                far_sent()
                pl.semaphore_signal(go, inc=1, device_id={"feat": mate}, device_id_type=MESH)

            @pl.when(jnp.logical_not(inner))
            def _():
                pl.semaphore_wait(go, 1)
                far("mask", 0).start()
                for t in range(pieces):
                    far("out", t).start()
                for i in range(chunks):
                    far("in", i, 0).start()
                    far("in", i, 1).start()

    def share(t, k):
        other = flip(me_f, t)
        return pltpu.make_async_remote_copy(
            src_ref=piece.at[k, other],
            dst_ref=landed.at[t, source(k)],
            send_sem=r_send.at[t, k],
            recv_sem=r_recv.at[t, k],
            device_id={"feat": other},
            device_id_type=MESH,
        )

    def score(k, c):
        blocks = [held[source(k), :, c * part + i].reshape(cols, width) for i in range(part)]
        span = slice(c * part * width, (c + 1) * part * width)
        got = lax.dot_general(
            q_buf[:, span], jnp.concatenate(blocks, axis=1), (((1,), (1,)), ((), ())), preferred_element_type=F32
        )
        if c > 0:
            got = acc[...] + got
        if c < chunks - 1:
            acc[...] = got
            return
        short = rows // fold
        for d in range(fn):
            cut = [got[d * rows + i * short:d * rows + (i + 1) * short] for i in range(fold)]
            piece[k, d] = jnp.concatenate(cut, axis=1).astype(piece.dtype)
        for t in range(fn - 1, 0, -1):
            share(t, k).start()
        landed[0, source(k)] = piece[k, me_f]

    def assemble(s):
        short = rows // fold
        total = landed[0, s].astype(F32)
        for t in range(1, fn):
            total = total + landed[t, s].astype(F32)
        for i in range(fold):
            for m in range(dn):
                at = (m * fn + s) * seqs
                out[i * short:(i + 1) * short, at:at + seqs] = total[:, i * cols + m * seqs:i * cols + (m + 1) * seqs]

    lags = [0] + [lag + n for n in range(last)]
    steps = len(events) + lags[-1]
    wide = min(feats, 1024)
    for e in range(steps):
        if e == lags[-1]:
            q_copy.wait()

            def reorder(i, carry):
                at = pl.ds(pl.multiple_of(i * wide, wide), wide)
                q_buf[:, at] = jnp.dot(perm[...], q_buf[:, at], preferred_element_type=F32).astype(BF16)
                return carry

            lax.fori_loop(0, feats // wide, reorder, 0)
        if relay and e == steps - 1:
            for k in range(fn - 1):
                for t in range(1, fn):
                    share(t, k).wait_recv()
            for s in (1, 2):
                assemble(s)
        for n in range(last + 1):
            if 0 <= e - lags[n] < len(events):
                stage(n, *events[e - lags[n]])
        if e >= lags[-1]:
            score(*events[e - lags[-1]])

    for k in range(fn - 1 if relay else 0, fn):
        for t in range(1, fn):
            share(t, k).wait_recv()
    for s in (0, 3) if relay else range(fn):
        assemble(s)

    for k in range(fn):
        for t in range(1, fn):
            share(t, k).wait_send()
    for k in range(1, 2 if relay else fn):
        for c in range(chunks):
            across(k, c).wait_send()
    if relay:
        @pl.when(inner)
        def _():
            for k in range(2, fn):
                for c in range(chunks):
                    across(k, c).wait_send()

        @pl.when(jnp.logical_not(inner))
        def _():
            far_sent()

    for k, c in events:
        for n, b in enumerate(bits):
            for m in masks_before(n):
                along(k, m, b, c).wait_send()


def local(fn, dn, layer_in, grad_out, in_proj, out_proj, queries, seq_ids, valid_counts, owner_order):
    tokens, model = layer_in.shape
    width = in_proj.shape[1]
    seqs = valid_counts.shape[0]
    q_rows, feats = queries.shape
    slab = width // fn
    rows = q_rows // fn
    chunks = max(1, min(4, slab // 16))
    tiles = max(1, min(2, tokens // 256))
    pieces = min(PIECES, tokens // 16)
    relay = fn == 4 and slab % 16 == 0
    fold = 2 if dn * seqs == 64 and rows % 32 == 0 else 1
    slots = 2 if relay else 1
    far_rows = slab if relay else 16
    dma = pltpu.SemaphoreType.DMA
    hbm = pl.BlockSpec(memory_space=pl.ANY)
    vmem = pl.BlockSpec(memory_space=pltpu.VMEM)
    return pl.pallas_call(
        functools.partial(kernel, fn, dn, chunks, tiles, pieces, LAG, fold, relay),
        out_shape=jax.ShapeDtypeStruct((rows, dn * fn * seqs), F32),
        in_specs=[hbm] * 5 + [vmem] * 3,
        out_specs=vmem,
        scratch_shapes=[
            pltpu.VMEM((tokens, model), BF16),
            pltpu.VMEM((tokens, model), BF16),
            pltpu.VMEM((model, width), BF16),
            pltpu.VMEM((model, width), BF16),
            pltpu.VMEM((q_rows, feats), BF16),
            pltpu.VMEM((width, tokens), BF16),
            pltpu.VMEM((tokens, width), BF16),
            pltpu.VMEM((seqs, tokens), BF16),
            pltpu.VMEM((fn - 1, slab, seqs, width), BF16),
            pltpu.VMEM((slots, tokens, width), BF16),
            pltpu.VMEM((slots, 2, far_rows, tokens), BF16),
            pltpu.VMEM((slots, seqs, tokens), BF16),
            pltpu.VMEM((fn, dn, slab, seqs, width), BF16),
            pltpu.VMEM((q_rows, dn * seqs), F32),
            pltpu.VMEM((q_rows, q_rows), BF16),
            pltpu.VMEM((fn, fn, rows // fold, fold * dn * seqs), BF16),
            pltpu.VMEM((fn, fn, rows // fold, fold * dn * seqs), BF16),
            dma((2,)),
            dma((tiles,)),
            dma((tiles,)),
            dma,
            dma((fn, chunks)),
            dma((fn, chunks)),
            dma((pieces + 1 + 2 * chunks,)),
            dma((slots, pieces + 1 + 2 * chunks)),
            dma((fn, dn, chunks)),
            dma((fn, dn, chunks)),
            dma((fn, fn)),
            dma((fn, fn)),
            pltpu.SemaphoreType.REGULAR,
        ],
        compiler_params=pltpu.CompilerParams(
            collective_id=0, has_side_effects=True, vmem_limit_bytes=VMEM
        ),
    )(layer_in, grad_out, in_proj, out_proj, queries, seq_ids, valid_counts.reshape(1, seqs), owner_order.reshape(1, q_rows))


def solution(mesh):
    in_specs = (
        P(("dom", "dp", "feat"), None),
        P(("dom", "dp", "feat"), None),
        P(),
        P(),
        P(("dom", "dp"), "feat"),
        P(("dom", "dp", "feat"), None),
        P(("dom", "dp", "feat")),
        P(("dom", "dp")),
    )
    out_specs = P(("dom", "dp", "feat"), None)
    body = functools.partial(local, mesh.shape["feat"], mesh.shape["dp"])
    return jax.shard_map(body, mesh=mesh, in_specs=in_specs, out_specs=out_specs, check_vma=False)
```
